32 devices in a mesh: seq: 4 (over y, x), tp: 8 (over z, core).
Axes of the slice: x: 2, y: 2, z: 4, core: 2. Of those that a mesh axis runs over, the one named last changes fastest.
Arguments:
- activations: bfloat16 [1024, 8192], P('seq', 'tp'), may hold values from -36 to 36
- norm_gain: bfloat16 [8192], P('tp'), may hold values from 0.099609375 to 1.8984375
- in_proj: bfloat16 [8192, 3, 4096], P(None, None, 'tp'), may hold values from -0.0625 to 0.0625
- short_taps: float32 [3, 3, 4096], P(None, None, 'tp'), may hold values from -3.5 to 3.5
- medium_taps: float32 [256, 128], P('tp'), may hold values from -0.5 to 0.5
- cotangent: bfloat16 [1024, 4096], P('seq', 'tp'), may hold values from -1.1953125 to 1.1953125
Outputs:
- mixer_out: bfloat16 [1024, 4096], P('seq', 'tp')
- grad_input: bfloat16 [1024, 8192], P('seq', 'tp')
- grad_proj: bfloat16 [8192, 3, 4096], P('seq', None, 'tp')
The draws below stay inside these ranges and needn't reach their ends.
All inputs are finite; a program needn't handle non-finite values.
Results may differ from the reference program's by a relative error of at most 0.02.
Values may be sent and summed in bfloat16 or wider, within the bound.
No kernel may reach another device: no remote copies, remote signals or barrier semaphores. Data moves between devices by JAX's collectives and lax.ppermute only.
A program may use at most 192 MiB of HBM per device.

```python
import math
import jax
import jax.numpy as jnp
from jax import lax

D = 8192
C = 4096
GROUP = 16
LS = 3
LM = 128
TOK_DEV = 256
TOKENS = 1024
GROUPS = 256
N_SEQ = 4


def draw_activations(key, part):
    base_key = jax.random.fold_in(key, 11)
    column_key = jax.random.fold_in(key, 12)
    row_key = jax.random.fold_in(key, 13)
    base = jnp.clip(jax.random.normal(base_key, (TOKENS, D), jnp.float32), -4.0, 4.0)
    columns = jnp.exp(jax.random.uniform(column_key, (1, D), jnp.float32, math.log(0.3), math.log(3.0)))
    row_scale = jnp.exp(jax.random.uniform(row_key, (TOKENS, 1), jnp.float32, math.log(0.3), math.log(3.0)))
    return (base * columns * row_scale).astype(jnp.bfloat16)


def shard_levels(own_key, extent, shards, least, largest):
    loudness = 1.0
    for dim, parts in shards:
        steps = jax.random.uniform(jax.random.fold_in(jax.random.fold_in(own_key, 6), dim), (parts,), jnp.float32, least / len(shards), largest / len(shards))
        loudness = loudness * jnp.repeat(jnp.exp(steps), extent[dim] // parts).reshape((-1,) + (1,) * (len(extent) - 1 - dim))
    return loudness


def bell_draw(rng, extent, deviation, reach, cuts=(), dtype=jnp.bfloat16):
    loudness = shard_levels(rng, extent, cuts, -0.22, 0.18) if cuts else 1.0
    result = jax.random.normal(rng, extent, jnp.float32) * deviation * loudness
    return jnp.minimum(jnp.maximum(result, -reach), reach).astype(dtype)


def setup_inputs(seed: int = 0) -> dict:
    arg_keys = jax.random.split(jax.random.key(seed), 7)
    return {
        "activations": draw_activations(jax.random.fold_in(arg_keys[6], 71), 0),
        "norm_gain": jnp.clip(1.0 + 0.18 * jax.random.normal(arg_keys[1], (D,), jnp.float32), 0.099609375, 1.8984375).astype(jnp.bfloat16),
        "in_proj": bell_draw(arg_keys[2], (D, 3, C), D ** -0.5, 0.0625, ((2, 8),)),
        "short_taps": bell_draw(arg_keys[3], (LS, 3, C), LS ** -0.5, 3.5, ((2, 8),), jnp.float32),
        "medium_taps": bell_draw(arg_keys[4], (GROUPS, LM), LM ** -0.5, 0.5, ((0, 8),), jnp.float32),
        "cotangent": bell_draw(arg_keys[5], (TOKENS, C), 0.2, 1.1953125, ((0, 4), (1, 8))),
    }


norm_eps = 1e-06

def causal_short(source, taps):
    length = source.shape[0]
    padded = jnp.concatenate([jnp.zeros((LS - 1,) + source.shape[1:], jnp.float32), source.astype(jnp.float32)], 0)
    total = jnp.zeros(source.shape, jnp.float32)
    for index in range(LS):
        total = total + taps[index] * padded[LS - 1 - index:LS - 1 - index + length]
    return total

def anticausal_short(source, taps):
    length = source.shape[0]
    padded = jnp.concatenate([source.astype(jnp.float32), jnp.zeros((LS - 1,) + source.shape[1:], jnp.float32)], 0)
    total = jnp.zeros(source.shape, jnp.float32)
    for index in range(LS):
        total = total + taps[index] * padded[index:index + length]
    return total

def causal_medium(source, tap_table):
    length = source.shape[0]
    padded = jnp.concatenate([jnp.zeros((LM - 1, source.shape[1]), jnp.float32), source.astype(jnp.float32)], 0)

    def add_tap(index, total):
        where_from = (LM - 1 - index).astype(jnp.int32)
        window = lax.dynamic_slice_in_dim(padded, where_from, length, 0)
        column = lax.dynamic_slice_in_dim(tap_table, index.astype(jnp.int32), 1, 1)[:, 0]
        return total + column * window
    return lax.fori_loop(0, LM, add_tap, jnp.zeros(source.shape, jnp.float32))

def anticausal_medium(source, tap_table):
    length = source.shape[0]
    padded = jnp.concatenate([source.astype(jnp.float32), jnp.zeros((LM - 1, source.shape[1]), jnp.float32)], 0)

    def add_tap(index, total):
        window = lax.dynamic_slice_in_dim(padded, index.astype(jnp.int32), length, 0)
        column = lax.dynamic_slice_in_dim(tap_table, index.astype(jnp.int32), 1, 1)[:, 0]
        return total + column * window
    return lax.fori_loop(0, LM, add_tap, jnp.zeros(source.shape, jnp.float32))

def reference(activations, norm_gain, in_proj, short_taps, medium_taps, cotangent):
    act_float = activations.astype(jnp.float32)
    inv_rms = lax.rsqrt(lax.optimization_barrier(jnp.mean(act_float * act_float, axis=1, keepdims=True)) + norm_eps)
    scaled = act_float * inv_rms
    gain_float = norm_gain.astype(jnp.float32)
    normed = (scaled * gain_float).astype(jnp.bfloat16)
    weight = in_proj.reshape(D, 3 * C)
    projected = jnp.dot(normed, weight, preferred_element_type=jnp.float32).astype(jnp.bfloat16).reshape(TOKENS, 3, C)
    feat = causal_short(projected, short_taps).astype(jnp.bfloat16)
    gated = (feat[:, 1].astype(jnp.float32) * feat[:, 2].astype(jnp.float32)).astype(jnp.bfloat16)
    tap_table = jnp.repeat(medium_taps, GROUP, axis=0)
    filtered = causal_medium(gated, tap_table)
    mixer_out = (feat[:, 0].astype(jnp.float32) * filtered).astype(jnp.bfloat16)
    grad_out = cotangent.astype(jnp.float32)
    grad_filtered = (grad_out * feat[:, 0].astype(jnp.float32)).astype(jnp.bfloat16)
    grad_gated = anticausal_medium(grad_filtered, tap_table)
    grad_q = grad_out * filtered
    grad_k = grad_gated * feat[:, 2].astype(jnp.float32)
    grad_v = grad_gated * feat[:, 1].astype(jnp.float32)
    grad_feat = jnp.stack([grad_q, grad_k, grad_v], 1).astype(jnp.bfloat16)
    grad_pre = anticausal_short(grad_feat, short_taps).astype(jnp.bfloat16).reshape(TOKENS, 3 * C)
    grad_normed = jnp.dot(grad_pre, weight.T, preferred_element_type=jnp.float32)
    grad_scaled = gain_float * grad_normed
    stat = lax.optimization_barrier(jnp.mean(grad_scaled * scaled, axis=1, keepdims=True))
    grad_input = (inv_rms * (grad_scaled - scaled * stat)).astype(jnp.bfloat16)
    normed_slabs = normed.reshape(N_SEQ, TOK_DEV, D)
    grad_slabs = grad_pre.reshape(N_SEQ, TOK_DEV, 3 * C)

    def add_slab(total, pair):
        slab_norm, slab_grad = pair
        partial_sum = jnp.dot(slab_norm.T, slab_grad, preferred_element_type=jnp.float32).astype(jnp.bfloat16)
        partial_sum = lax.optimization_barrier(partial_sum)
        return (total + partial_sum.astype(jnp.float32), None)
    total, _ = lax.scan(add_slab, jnp.zeros((D, 3 * C), jnp.float32), (normed_slabs, grad_slabs))
    grad_proj = total.astype(jnp.bfloat16).reshape(D, 3, C)
    return (mixer_out, grad_input, grad_proj)
```

```python
import jax
import jax.numpy as jnp
from jax import lax
from jax.experimental import pallas as pl
from jax.experimental.pallas import tpu as pltpu
from jax.sharding import PartitionSpec as P

GROUP = 16
LS = 3
LM = 128
EXTRA = 8

norm_eps = 1e-06


f32 = jnp.float32
bf16 = jnp.bfloat16


def band_body(taps_ref, rev_ref, fwd_ref, bwd_ref):
    row = lax.broadcasted_iota(jnp.int32, (LM, LM), 0)
    col = lax.broadcasted_iota(jnp.int32, (LM, LM), 1)
    upper = col >= row
    for g in range(taps_ref.shape[0]):
        taps = jnp.broadcast_to(taps_ref[g : g + 1, :], (LM, LM))
        rev = jnp.broadcast_to(rev_ref[g : g + 1, :], (LM, LM))
        across = pltpu.roll(taps, 0, 1, stride=1, stride_axis=0)
        along = pltpu.roll(rev, 0, 1, stride=1, stride_axis=0)
        fwd_ref[g, :LM, :] = jnp.where(upper, 0.0, across).astype(bf16)
        fwd_ref[g, LM:, :] = jnp.where(upper, across, 0.0).astype(bf16)
        keep = col <= row
        bwd_ref[g, :LM, :] = jnp.where(keep, along, 0.0).astype(bf16)
        bwd_ref[g, LM:, :] = jnp.where(keep, 0.0, along).astype(bf16)


def build_bands(medium_taps):
    groups = medium_taps.shape[0]
    reverse = jnp.roll(medium_taps[:, ::-1], 1, axis=1)
    per = 8
    spec = pl.BlockSpec((per, LM), lambda i: (i, 0))
    out = pl.BlockSpec((per, 2 * LM, LM), lambda i: (i, 0, 0))
    shape = jax.ShapeDtypeStruct((groups, 2 * LM, LM), bf16)
    return pl.pallas_call(
        band_body,
        grid=(groups // per,),
        in_specs=[spec, spec],
        out_specs=[out, out],
        out_shape=[shape, shape],
        name="bands",
    )(medium_taps, reverse)


def forward_call(info, line, pieces, weight, state, slots, sub_width):
    rows = pieces[0].shape[0] - EXTRA
    chunk = pieces[0].shape[1]
    branches, width, local_ch = weight.shape
    subs = chunk // sub_width
    count = len(pieces)
    first = state is None

    def body(info_ref, *refs):
        xs = refs[:count]
        w_ref = refs[count]
        rest = refs[count + 1 :]
        if first:
            acc_ref, ssq_ref, store_ref = rest
        else:
            acc_in, ssq_in, _, acc_ref, ssq_ref, store_ref = rest
        step = pl.program_id(0)

        @pl.when(step == 0)
        def _():
            if first:
                acc_ref[...] = jnp.zeros_like(acc_ref)
                ssq_ref[...] = jnp.zeros_like(ssq_ref)
            else:
                acc_ref[...] = acc_in[...]
                ssq_ref[...] = ssq_in[...]

        for which in range(count):
            @pl.when((step // subs == which) & (info_ref[line, count + which] > 0))
            def _(which=which):
                x_ref = xs[which]
                store_ref[0] = x_ref[...]
                x = x_ref[:rows, :].astype(f32)
                gain = x_ref[rows : rows + 1, :].astype(f32)
                sq = x * x
                part = sq[:, :128]
                for i in range(1, sub_width // 128):
                    part = part + sq[:, i * 128 : (i + 1) * 128]
                ssq_ref[...] += part
                xg = (x * gain).astype(bf16)
                for j in range(branches):
                    acc_ref[:, j * local_ch : (j + 1) * local_ch] += jnp.dot(
                        xg, w_ref[j], preferred_element_type=f32
                    )

    def x_spec(which):
        return pl.BlockSpec(
            (rows + EXTRA, sub_width),
            lambda i, info_ref: (0, jnp.clip(i - which * subs, 0, subs - 1)),
        )

    def w_map(i, info_ref):
        which = i // subs
        fresh = info_ref[line, which] * subs + i % subs
        kept = info_ref[line, 2 * count + which]
        return (0, jnp.where(info_ref[line, count + which] > 0, fresh, kept), 0)

    def store_map(i, info_ref):
        which = i // subs
        good = info_ref[line, count + which] > 0
        place = jnp.where(good, info_ref[line, which], slots - 1)
        return (place, 0, jnp.where(good, i % subs, 0))

    whole = lambda shape: pl.BlockSpec(shape, lambda i, info_ref: (0, 0))
    acc_shape = (rows, branches * local_ch)
    in_specs = [x_spec(w) for w in range(count)] + [
        pl.BlockSpec((branches, sub_width, local_ch), w_map)
    ]
    args = list(pieces) + [weight]
    aliases = {}
    if not first:
        in_specs += [whole(acc_shape), whole((rows, 128)), pl.BlockSpec(memory_space=pl.ANY)]
        args += list(state)
        aliases = {count + 2: 0, count + 3: 1, count + 4: 2}
    return pl.pallas_call(
        body,
        grid_spec=pltpu.PrefetchScalarGridSpec(
            num_scalar_prefetch=1,
            grid=(count * subs,),
            in_specs=in_specs,
            out_specs=[
                whole(acc_shape),
                whole((rows, 128)),
                pl.BlockSpec((1, rows + EXTRA, sub_width), store_map),
            ],
        ),
        out_shape=[
            jax.ShapeDtypeStruct(acc_shape, f32),
            jax.ShapeDtypeStruct((rows, 128), f32),
            jax.ShapeDtypeStruct((slots, rows + EXTRA, chunk), bf16),
        ],
        input_output_aliases=aliases,
        cost_estimate=pl.CostEstimate(
            flops=4 * rows * chunk * branches * local_ch,
            transcendentals=0,
            bytes_accessed=4 * chunk * branches * local_ch,
        ),
        name="project",
    )(info, *args)


def edges_call(acc, ssq, cotangent, taps, width):
    rows, total = acc.shape
    local_ch = total // 3

    def body(acc_ref, ssq_ref, cot_ref, taps_ref, pre_ref, inv_ref, right_ref, left_ref):
        mean = jnp.sum(ssq_ref[...], axis=1, keepdims=True) * (1.0 / width)
        inv = lax.rsqrt(mean + norm_eps)
        inv_ref[...] = jnp.broadcast_to(inv, (rows, 128))
        feats = []
        edge = []
        for j in range(3):
            cols = slice(j * local_ch, (j + 1) * local_ch)
            pre = (acc_ref[:, cols] * inv).astype(bf16)
            pre_ref[:, cols] = pre
            value = pre.astype(f32)
            edge.append((value[:8], value[rows - 8 :]))
            feat = taps_ref[j : j + 1, :] * value
            for i in range(1, LS):
                feat = feat + taps_ref[3 * i + j : 3 * i + j + 1, :] * pltpu.roll(value, i, 0)
            feats.append(feat.astype(bf16).astype(f32))
        row8 = lax.broadcasted_iota(jnp.int32, (8, local_ch), 0)
        gated = (feats[1] * feats[2]).astype(bf16)
        right_ref[:LM, :] = gated[rows - LM :]
        tail = jnp.where(
            row8 < 2,
            pltpu.roll(edge[0][1], 2, 0),
            jnp.where(row8 < 4, pltpu.roll(edge[1][1], 4, 0), pltpu.roll(edge[2][1], 6, 0)),
        )
        right_ref[LM:, :] = jnp.concatenate([tail, jnp.zeros_like(tail)], 0).astype(bf16)
        cot = cot_ref[...].astype(f32)
        grad = (cot * feats[0]).astype(bf16)
        left_ref[:LM, :] = grad[:LM]
        after = grad[LM : LM + 16].astype(f32)[:8]
        head = jnp.where(
            row8 < 2,
            after,
            jnp.where(
                row8 < 4,
                pltpu.roll(edge[0][0], 2, 0),
                jnp.where(row8 < 6, pltpu.roll(edge[1][0], 4, 0), pltpu.roll(edge[2][0], 6, 0)),
            ),
        )
        left_ref[LM:, :] = jnp.concatenate([head, cot[:8]], 0).astype(bf16)

    return pl.pallas_call(
        body,
        out_shape=[
            jax.ShapeDtypeStruct((rows, total), bf16),
            jax.ShapeDtypeStruct((rows, 128), f32),
            jax.ShapeDtypeStruct((LM + 16, local_ch), bf16),
            jax.ShapeDtypeStruct((LM + 16, local_ch), bf16),
        ],
        name="edges",
    )(acc, ssq, cotangent, taps)


def mixer_call(pre, inv, cotangent, from_prev, from_next, taps, fwd_band, bwd_band, width):
    rows, total = pre.shape
    local_ch = total // 3
    groups = local_ch // GROUP
    reach = rows + 8
    blocks = rows // LM

    def body(
        pre_ref, inv_ref, cot_ref, prev_ref, next_ref, taps_ref, fb_ref, bb_ref,
        out_ref, gps_ref, share_ref, ext, gate_t, grad_t, filt_t, back_t, feats, gfeat,
    ):
        row8 = lax.broadcasted_iota(jnp.int32, (8, local_ch), 0)
        prev_tail = prev_ref[LM:, :].astype(f32)[:8]
        next_all = next_ref[LM:, :].astype(f32)
        next_head, next_cot = next_all[:8], next_all[8:]
        for j in range(3):
            cols = slice(j * local_ch, (j + 1) * local_ch)
            ext[:8, :] = pltpu.roll(prev_tail, 6 - 2 * j, 0)
            ext[8 : rows + 8, :] = pre_ref[:, cols].astype(f32)
            ext[rows + 8 :, :] = pltpu.roll(next_head, 6 - 2 * j, 0)
            feat = taps_ref[j : j + 1, :] * ext[8 : 8 + reach, :]
            for i in range(1, LS):
                feat = feat + taps_ref[3 * i + j : 3 * i + j + 1, :] * ext[8 - i : 8 - i + reach, :]
            feats[j] = feat.astype(bf16).astype(f32)
        zero_rest = jnp.zeros((LM - 8, local_ch), f32)
        gated = feats[1] * feats[2]
        cot = cot_ref[...].astype(f32)
        grad = cot * feats[0, :rows]
        edge_grad = next_cot * feats[0, rows:]
        gate_t[:, :LM] = prev_ref[:LM, :].astype(f32).T.astype(bf16)
        for b in range(blocks):
            gate_t[:, (b + 1) * LM : (b + 2) * LM] = gated[b * LM : (b + 1) * LM].T.astype(bf16)
            grad_t[:, b * LM : (b + 1) * LM] = grad[b * LM : (b + 1) * LM].T.astype(bf16)
        gate_t[:, (blocks + 1) * LM :] = (
            jnp.concatenate([gated[rows:], zero_rest], 0).T.astype(bf16)
        )
        next_grad = next_ref[:LM, :].astype(f32)
        first8 = jnp.where(row8 < 2, edge_grad, next_grad[:8])
        grad_t[:, rows : rows + LM] = (
            jnp.concatenate([first8, next_grad[8:]], 0).T.astype(bf16)
        )
        last8 = jnp.where(row8 < 1, next_head, 0.0)
        grad_t[:, rows + LM :] = jnp.concatenate([last8, zero_rest], 0).T.astype(bf16)

        def one(g, _):
            at = pl.ds(pl.multiple_of(g * GROUP, GROUP), GROUP)
            for source, band, target in ((gate_t, fb_ref, filt_t), (grad_t, bb_ref, back_t)):
                strip = source[at, :]
                lhs = jnp.concatenate(
                    [strip[:, b * LM : (b + 2) * LM] for b in range(blocks + 1)], 0
                )
                res = jnp.dot(lhs, band[g], preferred_element_type=f32)
                for b in range(blocks + 1):
                    target[at, b * LM : (b + 1) * LM] = res[b * GROUP : (b + 1) * GROUP]
            return _

        lax.fori_loop(0, groups, one, 0, unroll=4)
        filtered = jnp.concatenate(
            [filt_t[:, b * LM : (b + 1) * LM].T for b in range(blocks)]
            + [filt_t[:, rows : rows + LM].T[:8]],
            0,
        )
        grad_gated = jnp.concatenate(
            [back_t[:, b * LM : (b + 1) * LM].T for b in range(blocks)]
            + [back_t[:, rows : rows + LM].T[:8]],
            0,
        )
        out_ref[...] = (feats[0, :rows] * filtered[:rows]).astype(bf16)
        cot_ext = jnp.concatenate([cot, next_cot], 0)
        inv = inv_ref[:, :1]
        share = jnp.zeros((rows, 128), f32)
        for j in range(3):
            cols = slice(j * local_ch, (j + 1) * local_ch)
            if j == 0:
                grad_feat = cot_ext * filtered
            else:
                grad_feat = grad_gated * feats[3 - j]
            gfeat[...] = grad_feat.astype(bf16).astype(f32)
            grad_pre = taps_ref[j : j + 1, :] * gfeat[:rows, :]
            for i in range(1, LS):
                grad_pre = grad_pre + taps_ref[3 * i + j : 3 * i + j + 1, :] * gfeat[i : i + rows, :]
            scaled = (grad_pre * inv).astype(bf16)
            gps_ref[:, cols] = scaled
            prod = scaled.astype(f32) * pre_ref[:, cols].astype(f32)
            for i in range(local_ch // 128):
                share = share + prod[:, i * 128 : (i + 1) * 128]
        summed = jnp.sum(share, axis=1, keepdims=True) * inv * (1.0 / width)
        share_ref[...] = jnp.broadcast_to(summed, (rows, 128))

    span = (blocks + 2) * LM
    reach_t = (blocks + 1) * LM
    return pl.pallas_call(
        body,
        out_shape=[
            jax.ShapeDtypeStruct((rows, local_ch), bf16),
            jax.ShapeDtypeStruct((rows, total), bf16),
            jax.ShapeDtypeStruct((rows, 128), f32),
        ],
        scratch_shapes=[
            pltpu.VMEM((rows + 16, local_ch), f32),
            pltpu.VMEM((local_ch, span), bf16),
            pltpu.VMEM((local_ch, span), bf16),
            pltpu.VMEM((local_ch, reach_t), f32),
            pltpu.VMEM((local_ch, reach_t), f32),
            pltpu.VMEM((3, reach, local_ch), f32),
            pltpu.VMEM((reach, local_ch), f32),
        ],
        name="mixer",
    )(pre, inv, cotangent, from_prev, from_next, taps, fwd_band, bwd_band)


def back_call(info, line, count, gps, share, weight, store, pair, moved, sub_width, final):
    rows = gps.shape[0]
    branches, width, local_ch = weight.shape
    chunk = store.shape[2]
    subs = chunk // sub_width
    n_pair = len(pair)
    n_moved = len(moved)

    def body(info_ref, gps_ref, share_ref, w_ref, x_ref, *refs):
        outs = refs[n_pair + n_moved :]
        slot = pl.program_id(0) // subs
        for which in range(count):
            @pl.when((slot == which) & (info_ref[line, count + which] > 0))
            def _(which=which):
                total = jnp.zeros((rows, sub_width), f32)
                for j in range(branches):
                    total = total + lax.dot_general(
                        gps_ref[:, j * local_ch : (j + 1) * local_ch],
                        w_ref[j],
                        (((1,), (1,)), ((), ())),
                        preferred_element_type=f32,
                    )
                x = x_ref[0, :rows, :].astype(f32)
                gain = x_ref[0, rows : rows + 1, :].astype(f32)
                total = gain * total - x * share_ref[:, :1]
                if n_pair:
                    total = total + refs[which][...].astype(f32)
                if n_moved:
                    chosen = range(n_moved) if count == 1 else [which]
                    for m in chosen:
                        total = total + refs[n_pair + m][...].astype(f32)
                outs[which][...] = total.astype(bf16)

    whole = lambda shape: pl.BlockSpec(shape, lambda i, info_ref: (0,) * len(shape))

    def by_slot(which):
        return pl.BlockSpec(
            (rows, sub_width),
            lambda i, info_ref: (0, jnp.clip(i - which * subs, 0, subs - 1)),
        )

    def block_of(i, info_ref):
        which = i // subs
        fresh = info_ref[line, which] * subs + i % subs
        kept = info_ref[line, 2 * count + which]
        return jnp.where(info_ref[line, count + which] > 0, fresh, kept)

    def x_map(i, info_ref):
        block = block_of(i, info_ref)
        return (block // subs, 0, block % subs)

    in_specs = [
        whole(gps.shape),
        whole(share.shape),
        pl.BlockSpec(
            (branches, sub_width, local_ch), lambda i, info_ref: (0, block_of(i, info_ref), 0)
        ),
        pl.BlockSpec((1, rows + EXTRA, sub_width), x_map),
    ]
    args = [gps, share, weight, store]
    for which, piece in enumerate(pair):
        in_specs.append(by_slot(which))
        args.append(piece)
    for which, piece in enumerate(moved):
        in_specs.append(by_slot(which if count > 1 else 0))
        args.append(piece)
    out = jax.ShapeDtypeStruct((rows, chunk), bf16)
    return pl.pallas_call(
        body,
        grid_spec=pltpu.PrefetchScalarGridSpec(
            num_scalar_prefetch=1,
            grid=(count * subs,),
            in_specs=in_specs,
            out_specs=[by_slot(which) for which in range(count)],
        ),
        out_shape=[out] * count,
        cost_estimate=pl.CostEstimate(
            flops=2 * rows * chunk * branches * local_ch,
            transcendentals=0,
            bytes_accessed=2 * chunk * branches * local_ch,
        ),
        name="back",
    )(info, *args)


def outer_call(info, line, store, mine, theirs, grads, tile):
    blocks = len(grads)
    rows, total = grads[0].shape
    chunk = store.shape[2]
    local_ch = total // 3
    tiles = chunk // tile

    def body(info_ref, own_ref, *refs):
        mine_refs = refs[: blocks - 1]
        their_refs = refs[blocks - 1 : 2 * blocks - 2]
        grad_refs = refs[2 * blocks - 2 : 3 * blocks - 2]
        out_ref, all_grads = refs[-2:]
        step = pl.program_id(0)

        @pl.when(step == 0)
        def _():
            for b in range(blocks):
                all_grads[b * rows : (b + 1) * rows, :] = grad_refs[b][...]

        gain = own_ref[0, rows : rows + 1, :].astype(f32)
        for side, others in ((0, mine_refs), (1, their_refs)):
            @pl.when(step // tiles == side)
            def _(others=others):
                parts = [own_ref[0, :rows, :]] + [ref[...] for ref in others]
                left = jnp.concatenate(
                    [(part.astype(f32) * gain).T.astype(bf16) for part in parts], 1
                )
                for j in range(3):
                    out_ref[j] = jnp.dot(
                        left,
                        all_grads[:, j * local_ch : (j + 1) * local_ch],
                        preferred_element_type=f32,
                    ).astype(bf16)

    def side_spec(side):
        return pl.BlockSpec(
            (rows, tile), lambda i, info_ref: (0, jnp.clip(i - side * tiles, 0, tiles - 1))
        )

    whole = pl.BlockSpec((rows, total), lambda i, info_ref: (0, 0))
    return pl.pallas_call(
        body,
        grid_spec=pltpu.PrefetchScalarGridSpec(
            num_scalar_prefetch=1,
            grid=(2 * tiles,),
            in_specs=[
                pl.BlockSpec(
                    (1, rows + EXTRA, tile),
                    lambda i, info_ref: (info_ref[line, i // tiles], 0, i % tiles),
                )
            ]
            + [side_spec(0)] * (blocks - 1)
            + [side_spec(1)] * (blocks - 1)
            + [whole] * blocks,
            out_specs=pl.BlockSpec(
                (3, tile, local_ch),
                lambda i, info_ref: (0, info_ref[line, 2 + i // tiles] * tiles + i % tiles, 0),
            ),
            scratch_shapes=[pltpu.VMEM((blocks * rows, total), bf16)],
        ),
        out_shape=jax.ShapeDtypeStruct((3, 2 * chunk, local_ch), bf16),
        cost_estimate=pl.CostEstimate(
            flops=4 * blocks * rows * chunk * total,
            transcendentals=0,
            bytes_accessed=4 * chunk * total,
        ),
        name="outer",
    )(info, store, *mine, *theirs, *grads)


def after(value, *others):
    return lax.optimization_barrier((value, others))[0]


def per_device(activations, norm_gain, in_proj, short_taps, medium_taps, cotangent):
    tp = lax.axis_size("tp")
    seq = lax.axis_size("seq")
    chips = tp // 2
    rank = lax.axis_index("tp")
    spot = lax.axis_index("seq")
    place, core = rank // 2, rank % 2
    rows, chunk = activations.shape
    width, _, local_ch = in_proj.shape
    slots = tp + 1
    sub_width = min(512, chunk)
    subs = chunk // sub_width
    weight = in_proj.transpose(1, 0, 2)
    taps = short_taps.reshape(LS * 3, local_ch)

    def send(value, routes):
        pairs = [(2 * a + c, 2 * b + c) for a, b in routes for c in range(2)]
        return lax.ppermute(value, "tp", pairs)

    def swap(value):
        return lax.ppermute(value, "tp", [(i, i ^ 1) for i in range(tp)])

    def chunk_of(chip, own):
        chip = jnp.clip(chip, 0, chips - 1)
        return 2 * chip + (core if own else 1 - core)

    lines = []

    def line_for(entries):
        chunks = [c for c, _ in entries]
        valid = [jnp.asarray(v, jnp.int32) for _, v in entries]
        kept = []
        for i in range(len(entries)):
            later = [n for n in range(i + 1, len(entries))]
            earlier = [n for n in range(i)]
            pick = chunks[i] * subs
            for n in reversed(later):
                pick = jnp.where(valid[n] > 0, chunks[n] * subs, pick)
            for n in earlier:
                pick = jnp.where(valid[n] > 0, chunks[n] * subs + subs - 1, pick)
            kept.append(pick)
        lines.append(chunks + valid + kept)
        return len(lines) - 1

    def merged(k):
        return 2 * k >= chips

    def joint(k):
        return 2 * k > chips + 1

    below_ok = [place >= k for k in range(chips)]
    above_ok = [place + k < chips for k in range(chips)]

    fwd_lines, part_lines, sent_lines = [], [], []
    for k in range(chips):
        low, high = place - k, place + k
        if k == 0:
            fwd_lines.append(line_for([(chunk_of(place, True), 1), (chunk_of(place, False), 1)]))
        elif merged(k):
            chip = jnp.where(below_ok[k], low, high)
            ok = below_ok[k] | above_ok[k]
            fwd_lines.append(line_for([(chunk_of(chip, True), ok), (chunk_of(chip, False), ok)]))
        else:
            fwd_lines.append(
                line_for(
                    [
                        (chunk_of(low, True), below_ok[k]), (chunk_of(low, False), below_ok[k]),
                        (chunk_of(high, True), above_ok[k]), (chunk_of(high, False), above_ok[k]),
                    ]
                )
            )
    for k in range(chips):
        for own, target in ((False, part_lines), (True, sent_lines)):
            low, high = place - k, place + k
            if k == 0:
                target.append(line_for([(chunk_of(place, own), 1)]))
            elif merged(k):
                chip = jnp.where(below_ok[k], low, high)
                target.append(line_for([(chunk_of(chip, own), below_ok[k] | above_ok[k])]))
            else:
                target.append(
                    line_for(
                        [(chunk_of(low, own), below_ok[k]), (chunk_of(high, own), above_ok[k])]
                    )
                )
    lines.append([2 * spot + core, 2 * spot + 1 - core, core, 1 - core])
    outer_line = len(lines) - 1
    longest = max(len(line) for line in lines)
    info = jnp.stack(
        [
            jnp.stack(
                [jnp.asarray(e, jnp.int32) for e in line]
                + [jnp.int32(0)] * (longest - len(line))
            )
            for line in lines
        ]
    )

    own = jnp.concatenate(
        [activations, jnp.broadcast_to(norm_gain[None, :], (EXTRA, chunk))], 0
    )
    up, down = (
        send(own, [(z, z + 1) for z in range(chips - 1)]),
        send(own, [(z, z - 1) for z in range(1, chips)]),
    )
    mate = swap(own)
    fwd_band, bwd_band = build_bands(medium_taps)
    own_late, fwd_band, bwd_band = lax.optimization_barrier((own, fwd_band, bwd_band))
    state = forward_call(info, fwd_lines[0], [own_late, mate], weight, None, slots, sub_width)
    single = None
    for k in range(1, chips):
        if k > 1:
            ups = [(z, z + 1) for z in range(k - 1, chips - 1)]
            downs = [(z, z - 1) for z in range(1, chips - k + 1)]
            if joint(k):
                single = send(single, ups + downs)
            elif merged(k - 1):
                up, down = send(single, ups), send(single, downs)
            else:
                up, down = send(up, ups), send(down, downs)
        if merged(k):
            if not joint(k):
                single = jnp.where(below_ok[k], up, down)
            single, state = lax.optimization_barrier((single, state))
            pieces = [single, swap(single)]
        else:
            up, down, state = lax.optimization_barrier((up, down, state))
            pieces = [up, swap(up), down, swap(down)]
        state = forward_call(info, fwd_lines[k], pieces, weight, state, slots, sub_width)
    acc, ssq, store = state

    pre, inv, to_next, to_prev = edges_call(acc, ssq, cotangent, taps, width)
    from_prev = lax.ppermute(to_next, "seq", [(i, i + 1) for i in range(seq - 1)])
    from_next = lax.ppermute(to_prev, "seq", [(i + 1, i) for i in range(seq - 1)])
    store, from_prev, from_next = lax.optimization_barrier((store, from_prev, from_next))

    def cols_of(target):
        picked = lax.dynamic_slice(
            store, (2 * target + core, 0, 0), (1, rows + EXTRA, chunk)
        )
        return picked[0, :rows]

    routes = [[(i, (i + shift) % seq) for i in range(seq)] for shift in range(1, seq)]
    mine = [
        lax.ppermute(cols_of((spot + shift) % seq), "seq", routes[shift - 1])
        for shift in range(1, seq)
    ]
    mixer_out, gps, share = mixer_call(
        pre, inv, cotangent, from_prev, from_next, taps, fwd_band, bwd_band, width
    )

    def back(line, count, pair, moved, final=False):
        return back_call(
            info, line, count, gps, share, weight, store, pair, moved, sub_width, final
        )

    def slots_of(k):
        return 1 if k == 0 or merged(k) else 2

    parts = {}
    far = chips - 1
    parts[far] = back(part_lines[far], slots_of(far), (), ())
    pairs = {far: [swap(p) for p in parts[far]]}
    gps_late = after(gps, *parts[far])
    grads = [gps] + [lax.ppermute(gps_late, "seq", route) for route in routes]
    for k in range(chips - 2, -1, -1):
        parts[k] = back(part_lines[k], slots_of(k), (), ())
        pairs[k] = [swap(p) for p in parts[k]]
    moved = ()
    for k in range(far, -1, -1):
        sent = back(sent_lines[k], slots_of(k), tuple(pairs[k]), moved, k == 0)
        if k == 0:
            grad_input = sent[0]
            break
        downs = [(z, z - 1) for z in range(k, chips)]
        ups = [(z, z + 1) for z in range(chips - k)]
        if joint(k):
            moved = (send(sent[0], downs + ups),)
        else:
            moved = (send(sent[0], downs), send(sent[-1], ups))
        if k == 1:
            late = after((tuple(grads), tuple(mine)), *sent)
            grads, mine = list(late[0]), list(late[1])

    theirs = [swap(m) for m in mine]
    grad_proj = outer_call(
        info, outer_line, store, mine, theirs, grads, min(256, chunk)
    ).transpose(1, 0, 2)
    return (mixer_out, grad_input, grad_proj)


def solution(mesh):
    return jax.shard_map(
        per_device,
        mesh=mesh,
        in_specs=(
            P("seq", "tp"),
            P("tp"),
            P(None, None, "tp"),
            P(None, None, "tp"),
            P("tp", None),
            P("seq", "tp"),
        ),
        out_specs=(P("seq", "tp"), P("seq", "tp"), P("seq", None, "tp")),
        check_vma=False,
    )
```

```python
import jax
import jax.numpy as jnp
from jax import lax
from jax.experimental import pallas as pl
from jax.experimental.pallas import tpu as pltpu
from jax.sharding import PartitionSpec as P

GROUP = 16
LS = 3
LM = 128
EXTRA = 8

norm_eps = 1e-06


f32 = jnp.float32
bf16 = jnp.bfloat16


def band_body(taps_ref, rev_ref, fwd_ref, bwd_ref):
    row = lax.broadcasted_iota(jnp.int32, (LM, LM), 0)
    col = lax.broadcasted_iota(jnp.int32, (LM, LM), 1)
    upper = col >= row
    for g in range(taps_ref.shape[0]):
        taps = jnp.broadcast_to(taps_ref[g : g + 1, :], (LM, LM))
        rev = jnp.broadcast_to(rev_ref[g : g + 1, :], (LM, LM))
        across = pltpu.roll(taps, 0, 1, stride=1, stride_axis=0)
        along = pltpu.roll(rev, 0, 1, stride=1, stride_axis=0)
        fwd_ref[g, :LM, :] = jnp.where(upper, 0.0, across).astype(bf16)
        fwd_ref[g, LM:, :] = jnp.where(upper, across, 0.0).astype(bf16)
        keep = col <= row
        bwd_ref[g, :LM, :] = jnp.where(keep, along, 0.0).astype(bf16)
        bwd_ref[g, LM:, :] = jnp.where(keep, 0.0, along).astype(bf16)


def build_bands(medium_taps):
    groups = medium_taps.shape[0]
    reverse = jnp.roll(medium_taps[:, ::-1], 1, axis=1)
    per = 8
    spec = pl.BlockSpec((per, LM), lambda i: (i, 0))
    out = pl.BlockSpec((per, 2 * LM, LM), lambda i: (i, 0, 0))
    shape = jax.ShapeDtypeStruct((groups, 2 * LM, LM), bf16)
    return pl.pallas_call(
        band_body,
        grid=(groups // per,),
        in_specs=[spec, spec],
        out_specs=[out, out],
        out_shape=[shape, shape],
        name="bands",
    )(medium_taps, reverse)


def pack_edges(acc_ref, ssq, cot_ref, taps_ref, pre_ref, inv_ref, right_ref, left_ref, width):
    rows, total = acc_ref.shape
    local_ch = total // 3
    mean = jnp.sum(ssq, axis=1, keepdims=True) * (1.0 / width)
    inv = lax.rsqrt(mean + norm_eps)
    inv_ref[...] = jnp.broadcast_to(inv, (rows, 128))
    feats = []
    edge = []
    for j in range(3):
        cols = slice(j * local_ch, (j + 1) * local_ch)
        pre = (acc_ref[:, cols] * inv).astype(bf16)
        pre_ref[:, cols] = pre
        value = pre.astype(f32)
        edge.append((value[:8], value[rows - 8 :]))
        feat = taps_ref[j : j + 1, :] * value
        for i in range(1, LS):
            feat = feat + taps_ref[3 * i + j : 3 * i + j + 1, :] * pltpu.roll(value, i, 0)
        feats.append(feat.astype(bf16).astype(f32))
    row8 = lax.broadcasted_iota(jnp.int32, (8, local_ch), 0)
    gated = (feats[1] * feats[2]).astype(bf16)
    right_ref[:LM, :] = gated[rows - LM :]
    tail = jnp.where(
        row8 < 2,
        pltpu.roll(edge[0][1], 2, 0),
        jnp.where(row8 < 4, pltpu.roll(edge[1][1], 4, 0), pltpu.roll(edge[2][1], 6, 0)),
    )
    right_ref[LM:, :] = jnp.concatenate([tail, jnp.zeros_like(tail)], 0).astype(bf16)
    cot = cot_ref[...].astype(f32)
    grad = (cot * feats[0]).astype(bf16)
    left_ref[:LM, :] = grad[:LM]
    after_rows = grad[LM : LM + 16].astype(f32)[:8]
    head = jnp.where(
        row8 < 2,
        after_rows,
        jnp.where(
            row8 < 4,
            pltpu.roll(edge[0][0], 2, 0),
            jnp.where(row8 < 6, pltpu.roll(edge[1][0], 4, 0), pltpu.roll(edge[2][0], 6, 0)),
        ),
    )
    left_ref[LM:, :] = jnp.concatenate([head, cot[:8]], 0).astype(bf16)


def forward_call(info, line, pieces, weight, state, slots, sub_width, tail=None):
    rows = pieces[0].shape[0] - EXTRA
    chunk = pieces[0].shape[1]
    branches, width, local_ch = weight.shape
    subs = chunk // sub_width
    count = len(pieces)
    first = state is None

    def body(info_ref, *refs):
        xs = refs[:count]
        w_ref = refs[count]
        rest = refs[count + 1 :]
        if first:
            acc_in = ssq_in = None
            acc_ref, ssq_ref, store_ref = rest
        elif tail is None:
            acc_in, ssq_in, _, acc_ref, ssq_ref, store_ref = rest
        else:
            acc_in, ssq_in, _, cot_ref, taps_ref = rest[:5]
            pre_ref, inv_ref, right_ref, left_ref, store_ref, acc_ref, ssq_ref = rest[5:]
        step = pl.program_id(0)

        @pl.when(step == 0)
        def _():
            if first:
                acc_ref[...] = jnp.zeros_like(acc_ref)
                ssq_ref[...] = jnp.zeros_like(ssq_ref)
            else:
                acc_ref[...] = acc_in[...]
                ssq_ref[...] = ssq_in[...]

        for which in range(count):
            @pl.when(step // subs == which)
            def _(which=which):
                x_ref = xs[which]
                store_ref[0] = x_ref[...]
                x = x_ref[:rows, :].astype(f32)
                gain = x_ref[rows : rows + 1, :].astype(f32)
                sq = x * x
                part = sq[:, :128]
                for i in range(1, sub_width // 128):
                    part = part + sq[:, i * 128 : (i + 1) * 128]
                ssq_ref[...] += part
                xg = (x * gain).astype(bf16)
                for j in range(branches):
                    acc_ref[:, j * local_ch : (j + 1) * local_ch] += jnp.dot(
                        xg, w_ref[j], preferred_element_type=f32
                    )

        if tail is not None:
            @pl.when(step == count * subs - 1)
            def _():
                pack_edges(
                    acc_ref, ssq_ref[...], cot_ref, taps_ref, pre_ref, inv_ref, right_ref,
                    left_ref, width,
                )

    def x_spec(which):
        return pl.BlockSpec(
            (rows + EXTRA, sub_width),
            lambda i, info_ref: (0, jnp.clip(i - which * subs, 0, subs - 1)),
        )

    def w_map(i, info_ref):
        return (0, info_ref[line, i // subs] * subs + i % subs, 0)

    def store_map(i, info_ref):
        return (info_ref[line, i // subs], 0, i % subs)

    whole = lambda shape: pl.BlockSpec(shape, lambda i, info_ref: (0, 0))
    acc_shape = (rows, branches * local_ch)
    ssq_shape = (rows, 128)
    in_specs = [x_spec(w) for w in range(count)] + [
        pl.BlockSpec((branches, sub_width, local_ch), w_map)
    ]
    args = list(pieces) + [weight]
    store_spec = pl.BlockSpec((1, rows + EXTRA, sub_width), store_map)
    store_shape = jax.ShapeDtypeStruct((slots, rows + EXTRA, chunk), bf16)
    aliases = {}
    scratch = []
    if not first:
        in_specs += [whole(acc_shape), whole(ssq_shape), pl.BlockSpec(memory_space=pl.ANY)]
        args += list(state)
    if tail is None:
        shapes = [(acc_shape, f32), (ssq_shape, f32)]
        if not first:
            aliases = {count + 2: 0, count + 3: 1, count + 4: 2}
    else:
        in_specs += [whole(t.shape) for t in tail]
        args += list(tail)
        edge = (LM + 16, local_ch)
        shapes = [(acc_shape, bf16), (ssq_shape, f32), (edge, bf16), (edge, bf16)]
        scratch = [pltpu.VMEM(acc_shape, f32), pltpu.VMEM(ssq_shape, f32)]
        aliases = {count + 4: 4}
    return pl.pallas_call(
        body,
        grid_spec=pltpu.PrefetchScalarGridSpec(
            num_scalar_prefetch=1,
            grid=(count * subs,),
            in_specs=in_specs,
            out_specs=[whole(shape) for shape, _ in shapes] + [store_spec],
            scratch_shapes=scratch,
        ),
        out_shape=[jax.ShapeDtypeStruct(shape, dtype) for shape, dtype in shapes] + [store_shape],
        input_output_aliases=aliases,
        cost_estimate=pl.CostEstimate(
            flops=4 * rows * chunk * branches * local_ch,
            transcendentals=0,
            bytes_accessed=4 * chunk * branches * local_ch,
        ),
        name="project",
    )(info, *args)


def mixer_call(pre, inv, cotangent, from_prev, from_next, taps, fwd_band, bwd_band, width):
    rows, total = pre.shape
    local_ch = total // 3
    groups = local_ch // GROUP
    reach = rows + 8
    blocks = rows // LM

    def body(
        pre_ref, inv_ref, cot_ref, prev_ref, next_ref, taps_ref, fb_ref, bb_ref,
        out_ref, gps_ref, share_ref, ext, gate_t, grad_t, filt_t, back_t, feats, gfeat,
    ):
        row8 = lax.broadcasted_iota(jnp.int32, (8, local_ch), 0)
        prev_tail = prev_ref[LM:, :].astype(f32)[:8]
        next_all = next_ref[LM:, :].astype(f32)
        next_head, next_cot = next_all[:8], next_all[8:]
        for j in range(3):
            cols = slice(j * local_ch, (j + 1) * local_ch)
            ext[:8, :] = pltpu.roll(prev_tail, 6 - 2 * j, 0)
            ext[8 : rows + 8, :] = pre_ref[:, cols].astype(f32)
            ext[rows + 8 :, :] = pltpu.roll(next_head, 6 - 2 * j, 0)
            feat = taps_ref[j : j + 1, :] * ext[8 : 8 + reach, :]
            for i in range(1, LS):
                feat = feat + taps_ref[3 * i + j : 3 * i + j + 1, :] * ext[8 - i : 8 - i + reach, :]
            feats[j] = feat.astype(bf16).astype(f32)
        zero_rest = jnp.zeros((LM - 8, local_ch), f32)
        gated = feats[1] * feats[2]
        cot = cot_ref[...].astype(f32)
        grad = cot * feats[0, :rows]
        edge_grad = next_cot * feats[0, rows:]
        gate_t[:, :LM] = prev_ref[:LM, :].astype(f32).T.astype(bf16)
        for b in range(blocks):
            gate_t[:, (b + 1) * LM : (b + 2) * LM] = gated[b * LM : (b + 1) * LM].T.astype(bf16)
            grad_t[:, b * LM : (b + 1) * LM] = grad[b * LM : (b + 1) * LM].T.astype(bf16)
        gate_t[:, (blocks + 1) * LM :] = (
            jnp.concatenate([gated[rows:], zero_rest], 0).T.astype(bf16)
        )
        next_grad = next_ref[:LM, :].astype(f32)
        first8 = jnp.where(row8 < 2, edge_grad, next_grad[:8])
        grad_t[:, rows : rows + LM] = (
            jnp.concatenate([first8, next_grad[8:]], 0).T.astype(bf16)
        )
        last8 = jnp.where(row8 < 1, next_head, 0.0)
        grad_t[:, rows + LM :] = jnp.concatenate([last8, zero_rest], 0).T.astype(bf16)

        def one(g, _):
            at = pl.ds(pl.multiple_of(g * GROUP, GROUP), GROUP)
            for source, band, target in ((gate_t, fb_ref, filt_t), (grad_t, bb_ref, back_t)):
                strip = source[at, :]
                lhs = jnp.concatenate(
                    [strip[:, b * LM : (b + 2) * LM] for b in range(blocks + 1)], 0
                )
                res = jnp.dot(lhs, band[g], preferred_element_type=f32)
                for b in range(blocks + 1):
                    target[at, b * LM : (b + 1) * LM] = res[b * GROUP : (b + 1) * GROUP]
            return _

        lax.fori_loop(0, groups, one, 0, unroll=4)
        filtered = jnp.concatenate(
            [filt_t[:, b * LM : (b + 1) * LM].T for b in range(blocks)]
            + [filt_t[:, rows : rows + LM].T[:8]],
            0,
        )
        grad_gated = jnp.concatenate(
            [back_t[:, b * LM : (b + 1) * LM].T for b in range(blocks)]
            + [back_t[:, rows : rows + LM].T[:8]],
            0,
        )
        out_ref[...] = (feats[0, :rows] * filtered[:rows]).astype(bf16)
        cot_ext = jnp.concatenate([cot, next_cot], 0)
        inv = inv_ref[:, :1]
        share = jnp.zeros((rows, 128), f32)
        for j in range(3):
            cols = slice(j * local_ch, (j + 1) * local_ch)
            if j == 0:
                grad_feat = cot_ext * filtered
            else:
                grad_feat = grad_gated * feats[3 - j]
            gfeat[...] = grad_feat.astype(bf16).astype(f32)
            grad_pre = taps_ref[j : j + 1, :] * gfeat[:rows, :]
            for i in range(1, LS):
                grad_pre = grad_pre + taps_ref[3 * i + j : 3 * i + j + 1, :] * gfeat[i : i + rows, :]
            scaled = (grad_pre * inv).astype(bf16)
            gps_ref[:, cols] = scaled
            prod = scaled.astype(f32) * pre_ref[:, cols].astype(f32)
            for i in range(local_ch // 128):
                share = share + prod[:, i * 128 : (i + 1) * 128]
        summed = jnp.sum(share, axis=1, keepdims=True) * inv * (1.0 / width)
        share_ref[...] = jnp.broadcast_to(summed, (rows, 128))

    span = (blocks + 2) * LM
    reach_t = (blocks + 1) * LM
    return pl.pallas_call(
        body,
        out_shape=[
            jax.ShapeDtypeStruct((rows, local_ch), bf16),
            jax.ShapeDtypeStruct((rows, total), bf16),
            jax.ShapeDtypeStruct((rows, 128), f32),
        ],
        scratch_shapes=[
            pltpu.VMEM((rows + 16, local_ch), f32),
            pltpu.VMEM((local_ch, span), bf16),
            pltpu.VMEM((local_ch, span), bf16),
            pltpu.VMEM((local_ch, reach_t), f32),
            pltpu.VMEM((local_ch, reach_t), f32),
            pltpu.VMEM((3, reach, local_ch), f32),
            pltpu.VMEM((reach, local_ch), f32),
        ],
        name="mixer",
    )(pre, inv, cotangent, from_prev, from_next, taps, fwd_band, bwd_band)


def back_call(info, line, gps, share, weight, store, sub_width, earlier=None):
    rows = gps.shape[0]
    branches, width, local_ch = weight.shape
    chunk = store.shape[2]
    subs = chunk // sub_width
    steps = 2 * subs
    share_rows = rows // steps

    def body(info_ref, gps_ref, share_ref, w_ref, x_ref, *refs):
        slot = pl.program_id(0) // subs
        total = jnp.zeros((rows, sub_width), f32)
        for j in range(branches):
            total = total + lax.dot_general(
                gps_ref[:, j * local_ch : (j + 1) * local_ch],
                w_ref[j],
                (((1,), (1,)), ((), ())),
                preferred_element_type=f32,
            )
        x = x_ref[0, :rows, :].astype(f32)
        gain = x_ref[0, rows : rows + 1, :].astype(f32)
        value = (gain * total - x * share_ref[:, :1]).astype(bf16)
        outs = refs if earlier is None else refs[2:]
        for which in range(2):
            @pl.when(slot == which)
            def _(which=which):
                outs[which][...] = value
        if earlier is not None:
            outs[2][...] = (refs[0][...].astype(f32) + refs[1][...].astype(f32)).astype(bf16)

    whole = lambda shape: pl.BlockSpec(shape, lambda i, info_ref: (0,) * len(shape))

    def by_slot(which):
        return pl.BlockSpec(
            (rows, sub_width),
            lambda i, info_ref: (0, jnp.clip(i - which * subs, 0, subs - 1)),
        )

    by_rows = pl.BlockSpec((share_rows, chunk), lambda i, info_ref: (i, 0))
    extra = [] if earlier is None else list(earlier)
    out = jax.ShapeDtypeStruct((rows, chunk), bf16)
    return pl.pallas_call(
        body,
        grid_spec=pltpu.PrefetchScalarGridSpec(
            num_scalar_prefetch=1,
            grid=(steps,),
            in_specs=[
                whole(gps.shape),
                whole(share.shape),
                pl.BlockSpec(
                    (branches, sub_width, local_ch),
                    lambda i, info_ref: (0, info_ref[line, i // subs] * subs + i % subs, 0),
                ),
                pl.BlockSpec(
                    (1, rows + EXTRA, sub_width),
                    lambda i, info_ref: (info_ref[line, i // subs], 0, i % subs),
                ),
            ]
            + [by_rows] * len(extra),
            out_specs=[by_slot(0), by_slot(1)] + [by_rows] * (len(extra) // 2),
        ),
        out_shape=[out] * (2 + len(extra) // 2),
        cost_estimate=pl.CostEstimate(
            flops=4 * rows * chunk * branches * local_ch,
            transcendentals=0,
            bytes_accessed=4 * chunk * branches * local_ch,
        ),
        name="back",
    )(info, gps, share, weight, store, *extra)


def outer_call(info, line, store, mine, theirs, grads, tile, own, partial):
    blocks = len(grads)
    lead = 1 if own else 0
    others = blocks - lead
    rows, total = grads[0].shape
    chunk = store.shape[2]
    local_ch = total // 3
    tiles = chunk // tile

    def body(info_ref, own_ref, *refs):
        mine_refs = refs[:others]
        their_refs = refs[others : 2 * others]
        grad_refs = refs[2 * others : 2 * others + blocks]
        out_ref, all_grads = refs[-2:]
        step = pl.program_id(0)

        @pl.when(step == 0)
        def _():
            for b in range(blocks):
                all_grads[b * rows : (b + 1) * rows, :] = grad_refs[b][...]

        gain = own_ref[0, rows : rows + 1, :].astype(f32)
        for side, moved in ((0, mine_refs), (1, their_refs)):
            @pl.when(step // tiles == side)
            def _(moved=moved):
                parts = [own_ref[0, :rows, :]] * lead + [ref[...] for ref in moved]
                left = jnp.concatenate(
                    [(part.astype(f32) * gain).T.astype(bf16) for part in parts], 1
                )
                for j in range(3):
                    value = jnp.dot(
                        left,
                        all_grads[:, j * local_ch : (j + 1) * local_ch],
                        preferred_element_type=f32,
                    )
                    if partial is not None:
                        value = value + refs[2 * others + blocks][j].astype(f32)
                    out_ref[j] = value.astype(bf16)

    def side_spec(side):
        return pl.BlockSpec(
            (rows, tile), lambda i, info_ref: (0, jnp.clip(i - side * tiles, 0, tiles - 1))
        )

    whole = pl.BlockSpec((rows, total), lambda i, info_ref: (0, 0))
    out_spec = pl.BlockSpec(
        (3, tile, local_ch),
        lambda i, info_ref: (0, info_ref[line, 2 + i // tiles] * tiles + i % tiles, 0),
    )
    extra = [] if partial is None else [partial]
    return pl.pallas_call(
        body,
        grid_spec=pltpu.PrefetchScalarGridSpec(
            num_scalar_prefetch=1,
            grid=(2 * tiles,),
            in_specs=[
                pl.BlockSpec(
                    (1, rows + EXTRA, tile),
                    lambda i, info_ref: (info_ref[line, i // tiles], 0, i % tiles),
                )
            ]
            + [side_spec(0)] * others
            + [side_spec(1)] * others
            + [whole] * blocks
            + [out_spec] * len(extra),
            out_specs=out_spec,
            scratch_shapes=[pltpu.VMEM((blocks * rows, total), bf16)],
        ),
        out_shape=jax.ShapeDtypeStruct((3, 2 * chunk, local_ch), bf16),
        cost_estimate=pl.CostEstimate(
            flops=4 * blocks * rows * chunk * total,
            transcendentals=0,
            bytes_accessed=4 * chunk * total,
        ),
        name="outer",
    )(info, store, *mine, *theirs, *grads, *extra)


def mixer_step(activations, norm_gain, in_proj, short_taps, medium_taps, cotangent):
    tp = lax.axis_size("tp")
    seq = lax.axis_size("seq")
    chips = tp // 2
    rank = lax.axis_index("tp")
    spot = lax.axis_index("seq")
    place, core = rank // 2, rank % 2
    rows, chunk = activations.shape
    width, _, local_ch = in_proj.shape
    wide = min(1024, chunk)
    narrow = min(512, chunk)
    weight = in_proj.transpose(1, 0, 2)
    taps = short_taps.reshape(LS * 3, local_ch)

    def send(value, r):
        pairs = [(2 * z + c, 2 * (z ^ r) + c) for z in range(chips) for c in range(2)]
        return lax.ppermute(value, "tp", pairs)

    def swap(value):
        return lax.ppermute(value, "tp", [(i, i ^ 1) for i in range(tp)])

    lines = []
    for r in range(chips):
        chip = place ^ r
        lines.append([2 * chip + core, 2 * chip + 1 - core, 0, 0])
    for r in range(chips):
        chip = place ^ r
        lines.append([2 * chip + 1 - core, 2 * chip + core, 0, 0])
    lines.append([2 * spot + core, 2 * spot + 1 - core, core, 1 - core])
    outer_line = len(lines) - 1
    info = jnp.stack([jnp.stack([jnp.asarray(e, jnp.int32) for e in line]) for line in lines])

    own = jnp.concatenate(
        [activations, jnp.broadcast_to(norm_gain[None, :], (EXTRA, chunk))], 0
    )
    mate = swap(own)
    arrived = []
    for r in range(1, chips):
        arrived.append(send(own, r))
    fwd_band, bwd_band = build_bands(medium_taps)
    own_late, fwd_band, bwd_band = lax.optimization_barrier((own, fwd_band, bwd_band))
    state = forward_call(info, 0, [own_late, mate], weight, None, tp, wide)
    for r in range(1, chips):
        piece = arrived[r - 1]
        tail = (cotangent, taps) if r == chips - 1 else None
        mate = swap(piece)
        state = forward_call(info, r, [piece, mate], weight, state, tp, wide, tail)
    pre, inv, to_next, to_prev, store = state
    from_prev = lax.ppermute(to_next, "seq", [(i, i + 1) for i in range(seq - 1)])
    from_next = lax.ppermute(to_prev, "seq", [(i + 1, i) for i in range(seq - 1)])

    def cols_of(target):
        picked = lax.dynamic_slice(
            store, (2 * target + core, 0, 0), (1, rows + EXTRA, chunk)
        )
        return picked[0, :rows]

    routes = [[(i, (i + shift) % seq) for i in range(seq)] for shift in range(1, seq)]
    mine = []
    for shift in range(1, seq):
        mine.append(lax.ppermute(cols_of((spot + shift) % seq), "seq", routes[shift - 1]))
    mixer_out, gps, share = mixer_call(
        pre, inv, cotangent, from_prev, from_next, taps, fwd_band, bwd_band, width
    )

    landed = []
    earlier = None
    for r in range(chips - 1, -1, -1):
        results = back_call(
            info, chips + r, gps, share, weight, store, narrow, earlier
        )
        if earlier is not None:
            landed.append(send(results[2], r + 1))
        pair = swap(results[0])
        if r == chips - 1:
            both = results[1].astype(f32) + pair.astype(f32)
            landed.append(send(both.astype(bf16), r))
        else:
            earlier = (results[1], pair)
    total = earlier[0].astype(f32) + earlier[1].astype(f32)
    for value in landed:
        total = total + value.astype(f32)
    grad_input = total.astype(bf16)

    grads = [gps]
    for shift in range(1, seq):
        grads.append(lax.ppermute(gps, "seq", routes[shift - 1]))
    theirs = [swap(m) for m in mine]
    tile = min(256, chunk)
    grad_proj = outer_call(
        info, outer_line, store, mine, theirs, grads, tile, True, None
    ).transpose(1, 0, 2)
    return (mixer_out, grad_input, grad_proj)


def solution(mesh):
    return jax.shard_map(
        mixer_step,
        mesh=mesh,
        in_specs=(
            P("seq", "tp"),
            P("tp"),
            P(None, None, "tp"),
            P(None, None, "tp"),
            P("tp", None),
            P("seq", "tp"),
        ),
        out_specs=(P("seq", "tp"), P("seq", "tp"), P("seq", None, "tp")),
        check_vma=False,
    )
```
